32 devices in a mesh: aux: 16 (over z, y, x), grp: 2 (over core).
Axes of the slice: x: 2, y: 2, z: 4, core: 2. Of those that a mesh axis runs over, the one named last changes fastest.
Arguments:
- integrals: bfloat16 [1024, 16, 4096], P(('aux', 'grp')), may hold values from -6 to 6
- block_pairs: int32 [32, 16, 2], P(('aux', 'grp')), may hold values from 0 to 63
- occupied: bfloat16 [2, 4096], replicated, may hold values from -0.75 to 0.75
- virtual: bfloat16 [4096, 3072], P(None, 'grp'), may hold values from -0.1875 to 0.1875
- stored: bfloat16 [1024, 6144], P('aux'), may hold values from -0.1875 to 0.1875
Outputs:
- exchange_panel: bfloat16 [2, 3072, 2, 3072], P(None, ('grp', 'aux'))
The draws below stay inside these ranges and needn't reach their ends.
Inputs may be any that keep to these rules, and one draw needn't show every extreme that they name: `block_pairs`: block pairs may repeat within a shard; repeated blocks add.
All inputs are finite; a program needn't handle non-finite values.
Results may differ from the reference program's by a relative error of at most 0.0095.
Values may be sent and summed in bfloat16 or wider, within the bound.
A program may use at most 192 MiB of HBM per device.

```python
import jax
import jax.numpy as jnp
from jax import lax

NBAS = 4096
BLK = 64
V = 3072
NOCC = 2
JWIN = 2
AUX_DEV = 32
NB = 16
SHARDS = 32
NAUX = 1024
N_AUX = 16
N_GRP = 2


def place_ends(entries, key, low, largest):
    index_at = [jax.random.randint(jax.random.fold_in(key, axis), (), 0, length) for axis, length in enumerate(entries.shape)]
    widest = entries.shape.index(max(entries.shape))
    neighbour = index_at[:widest] + [(index_at[widest] + 1) % entries.shape[widest]] + index_at[widest + 1:]
    return entries.at[tuple(index_at)].set(low).at[tuple(neighbour)].set(largest)


def block_scale(rng, shape, split, least, high):
    loudness = 1.0
    for dim, blocks in split:
        heights = jax.random.uniform(jax.random.fold_in(jax.random.fold_in(rng, 6), dim), (blocks,), jnp.float32, least / len(split), high / len(split))
        loudness = loudness * jnp.repeat(jnp.exp(heights), shape[dim] // blocks).reshape((-1,) + (1,) * (len(shape) - 1 - dim))
    return loudness


def centred(rng, dims, spread, bound, pieces=(), held_as=jnp.bfloat16):
    values = jax.random.normal(rng, dims, jnp.float32) * spread
    if len(pieces) > 0:
        values = block_scale(rng, dims, pieces, -0.22, 0.18) * values
    return jnp.clip(values, min=-bound, max=bound).astype(held_as)


def setup_inputs(seed: int = 0) -> dict:
    splits = jax.random.split(jax.random.key(seed), 6)
    integrals = centred(splits[0], (NAUX, NB, BLK * BLK), 1.0, 6.0, ((0, 32),))
    block_pairs = place_ends(jax.random.randint(splits[1], (SHARDS, NB, 2), 0, NBAS // BLK), jax.random.fold_in(splits[1], 1), 0, (NBAS // BLK) - 1).astype(jnp.int32)
    occupied = centred(splits[2], (NOCC, NBAS), BLK ** -0.5, 0.75)
    virtual = centred(splits[3], (NBAS, V), (BLK * NB) ** -0.5, 0.1875, ((1, 2),))
    stored = centred(splits[4], (NAUX, JWIN * V), NAUX ** -0.5, 0.1875, ((0, 16),))
    return dict(integrals=integrals, block_pairs=block_pairs, occupied=occupied, virtual=virtual, stored=stored)


def shard_factor(tiles, pairs, occupied, virtual):
    nblocks = NBAS // BLK
    block_iota = jnp.arange(nblocks, dtype=jnp.int32)
    row_pick = (pairs[:, 0:1] == block_iota[None, :]).astype(jnp.float32)
    col_pick = (pairs[:, 1:2] == block_iota[None, :]).astype(jnp.float32)
    occ_blocks = occupied.astype(jnp.float32).reshape(NOCC, nblocks, BLK)
    picked = jnp.einsum('ikm,bk->ibm', occ_blocks, row_pick)
    squares = tiles.astype(jnp.float32).reshape(AUX_DEV, NB, BLK, BLK)
    partial_value = jnp.einsum('ibm,pbmn->pibn', picked, squares)
    half = jnp.einsum('pibn,bk->pikn', partial_value, col_pick).reshape(AUX_DEV * NOCC, NBAS).astype(jnp.bfloat16)
    factor = jnp.dot(half, virtual, preferred_element_type=jnp.float32).astype(jnp.bfloat16)
    return factor.reshape(AUX_DEV, NOCC, V).transpose(0, 2, 1).reshape(AUX_DEV, V * NOCC)


def reference(integrals, block_pairs, occupied, virtual, stored):
    shard_count = N_AUX * N_GRP
    tiles_all = integrals.reshape(shard_count, AUX_DEV, NB, BLK * BLK)
    stored_all = stored.reshape(shard_count, AUX_DEV, JWIN * V)

    def step(carry, inputs):
        tiles, pairs, rows = inputs
        factor = shard_factor(tiles, pairs, occupied, virtual)
        term = lax.dot_general(factor, rows, (((0,), (0,)), ((), ())), preferred_element_type=jnp.float32)
        return carry + term, None

    start = jnp.zeros((V * NOCC, JWIN * V), jnp.float32)
    total, unused = lax.scan(step, start, (tiles_all, block_pairs, stored_all))
    result = total.astype(jnp.bfloat16).reshape(V, NOCC, JWIN, V)
    return result.transpose(1, 0, 2, 3)
```

```python
import functools

import jax
import jax.numpy as jnp
from jax import lax
from jax.experimental import pallas as pl
from jax.experimental.pallas import tpu as pltpu
from jax.sharding import PartitionSpec as P

MESH = pl.DeviceIdType.MESH
LANES = 128
PLANE = 4


def contract_kernel(blk, integrals, weights, out):
    nocc = weights.shape[0]
    for p in range(integrals.shape[0]):
        for i in range(nocc):
            total = None
            for t in range(integrals.shape[2] // LANES):
                cols = slice(t * LANES, (t + 1) * LANES)
                term = integrals[p, :, cols].astype(jnp.float32) * weights[i, :, cols]
                total = term if total is None else total + term
            part = total[:, :blk]
            for f in range(1, LANES // blk):
                part = part + total[:, f * blk:(f + 1) * blk]
            out[i, p] = part.astype(out.dtype)


def contract(integrals, weights, blk):
    aux_rows, nb, flat = integrals.shape
    nocc = weights.shape[0]
    step = 8
    return pl.pallas_call(
        functools.partial(contract_kernel, blk),
        grid=(aux_rows // step,),
        in_specs=[
            pl.BlockSpec((step, nb, flat), lambda p: (p, 0, 0)),
            pl.BlockSpec((nocc, nb, flat), lambda p: (0, 0, 0)),
        ],
        out_specs=pl.BlockSpec((nocc, step, nb, blk), lambda p: (0, p, 0, 0)),
        out_shape=jax.ShapeDtypeStruct((nocc, aux_rows, nb, blk), jnp.bfloat16),
    )(integrals, weights)


def factor_kernel(group, columns, parts, *refs):
    del columns
    slabs, out, total = refs[:group], refs[group], refs[group + 1]
    step = pl.program_id(1)

    @pl.when(step == 0)
    def _():
        total[...] = jnp.zeros_like(total)

    acc = total[...]
    for q in range(group):
        acc += jnp.dot(parts[0, q], slabs[q][...], preferred_element_type=jnp.float32)
    total[...] = acc

    @pl.when(step == pl.num_programs(1) - 1)
    def _():
        out[0] = acc.astype(out.dtype)


def factors(parts, columns, virtual):
    shards, nb, rows, blk = parts.shape
    slab = virtual.shape[1]
    group = 8
    slab_specs = [
        pl.BlockSpec((blk, slab), lambda s, k, idx, q=q: (idx[s * nb + k * group + q], 0))
        for q in range(group)
    ]
    return pl.pallas_call(
        functools.partial(factor_kernel, group),
        grid_spec=pltpu.PrefetchScalarGridSpec(
            num_scalar_prefetch=1,
            grid=(shards, nb // group),
            in_specs=[pl.BlockSpec((1, group, rows, blk), lambda s, k, idx: (s, k, 0, 0))]
            + slab_specs,
            out_specs=pl.BlockSpec((1, rows, slab), lambda s, k, idx: (s, 0, 0)),
            scratch_shapes=[pltpu.VMEM((rows, slab), jnp.float32)],
        ),
        out_shape=jax.ShapeDtypeStruct((shards, rows, slab), jnp.bfloat16),
    )(columns, parts, *([virtual] * group))


def panel_kernel(n_aux, n_grp, stored, chunk, out, rows, fac, total, block,
                 own_sem, recv, send, frecv, fsend, precv, psend, orecv, osend):
    me = lax.axis_index("aux")
    grp = lax.axis_index("grp")
    line = n_aux // PLANE
    width = rows.shape[2]
    cut = width // 3 // LANES * LANES
    spans = ((0, cut), (cut, width - cut))
    z = me // PLANE
    su = 1 + grp % 2
    sv = 3 - su
    u = (me // su) % 2
    v = (me // sv) % 2
    next_u = me + su * (1 - 2 * u)
    next_v = me + sv * (1 - 2 * v)
    up, down = z + 1 < line, z >= 1
    targets = {"up": me + PLANE, "down": me - PLANE, "u": next_u, "v": next_v}
    slots = {"up": 0, "down": 1, "u": 2, "v": 3}

    load = pltpu.make_async_copy(
        stored.at[:, pl.ds(pl.multiple_of(grp * width, LANES), width)], rows.at[me], own_sem.at[0])
    load.start()
    mine = pltpu.make_async_copy(chunk.at[me], fac.at[grp, me], own_sem.at[1])
    mine.start()

    barrier = pltpu.get_barrier_semaphore()
    for o in range(1, n_aux):
        pl.semaphore_signal(barrier, inc=1, device_id=(lax.rem(me + o, n_aux), grp), device_id_type=MESH)
    for o in range(1, n_grp):
        pl.semaphore_signal(barrier, inc=1, device_id=(me, lax.rem(grp + o, n_grp)), device_id_type=MESH)
    pl.semaphore_wait(barrier, n_aux - 1 + n_grp - 1)

    def copy(source, colour, way):
        at = rows.at[source, :, pl.ds(*spans[colour])]
        return pltpu.make_async_remote_copy(
            src_ref=at, dst_ref=at,
            send_sem=send.at[colour, slots[way], source], recv_sem=recv.at[colour, source],
            device_id=(targets[way], grp), device_id_type=MESH)

    def when(condition, action):
        if condition is None:
            action()
        else:
            pl.when(condition)(action)

    edges = {"up": up, "down": down, "u": None, "v": None}

    def ways_of(dz, du, dv, colour):
        if dv:
            return ()
        along = ("up", "down") if dz == 0 else (("up",) if dz > 0 else ("down",))
        if colour == 0:
            return ("v",) if du else along + ("u", "v")
        if dz == 0 and du == 0:
            return ("u",) + along + ("v",)
        return along + ("v",)

    def source_of(dz, du, dv):
        return (z - dz) * PLANE + su * (u + du * (1 - 2 * u)) + sv * (v + dv * (1 - 2 * v))

    def valid(dz):
        if dz == 0:
            return None
        return z - dz >= 0 if dz > 0 else z - dz < line

    sent = []

    def forward(dz, du, dv):
        source = source_of(dz, du, dv)
        for colour in (0, 1):
            ways = ways_of(dz, du, dv, colour)
            sent.append((dz, source, colour, ways))

            def act(colour=colour, ways=ways):
                if (dz, du, dv) != (0, 0, 0):
                    copy(source, colour, "v").wait_recv()
                for way in ways:
                    when(edges[way], copy(source, colour, way).start)

            when(valid(dz), act)

    def plane_dot(dz, first):
        def act():
            base = (z - dz) * PLANE
            tile = 512 if width % 512 == 0 else LANES

            @pl.loop(0, width // tile)
            def _(t):
                cols = pl.ds(pl.multiple_of(t * tile, tile), tile)
                right = rows[pl.ds(base, PLANE), :, cols].reshape(-1, tile)
                for q in range(n_grp):
                    left = fac[q, pl.ds(base, PLANE)].reshape(-1, fac.shape[3])
                    term = lax.dot_general(
                        left, right, (((0,), (0,)), ((), ())), preferred_element_type=jnp.float32)
                    if first:
                        total[q, :, cols] = term
                    else:
                        total[q, :, cols] += term

        when(valid(dz), act)

    offsets = [(dz, du, dv) for dz in range(1 - line, line) for du in (0, 1) for dv in (0, 1)]
    hops = lambda o: abs(o[0]) + o[1] + o[2]
    last_hop = line + 1

    def fac_copy(o):
        to = lax.rem(me + o, n_aux)
        return pltpu.make_async_remote_copy(
            src_ref=chunk.at[to], dst_ref=fac.at[grp, me], send_sem=fsend.at[o], recv_sem=frecv.at[o],
            device_id=(to, grp), device_id_type=MESH)

    def fac_wait(o):
        source = lax.rem(me + n_aux - o, n_aux)
        pltpu.make_async_remote_copy(
            src_ref=chunk.at[0], dst_ref=fac.at[grp, source], send_sem=fsend.at[o], recv_sem=frecv.at[o],
            device_id=(source, grp), device_id_type=MESH).wait_recv()
        return source

    def share(o, source, p):
        return pltpu.make_async_remote_copy(
            src_ref=fac.at[grp, source], dst_ref=fac.at[grp, source],
            send_sem=psend.at[p, o], recv_sem=precv.at[p, o],
            device_id=(me, lax.rem(grp + p, n_grp)), device_id_type=MESH)

    for hop in range(last_hop + 1):
        if hop == 0:
            load.wait()
        for offset in offsets:
            if hops(offset) == hop:
                forward(*offset)
        if hop == 0:
            for o in range(1, n_aux):
                fac_copy(o).start()
            mine.wait()
        if hop == 1:
            for o in range(n_aux):
                source = me if o == 0 else fac_wait(o)
                for p in range(1, n_grp):
                    share(o, source, p).start()
            for o in range(n_aux):
                source = lax.rem(me + n_aux - o, n_aux)
                for p in range(1, n_grp):
                    giver = lax.rem(grp + n_grp - p, n_grp)
                    pltpu.make_async_remote_copy(
                        src_ref=fac.at[grp, source], dst_ref=fac.at[giver, source],
                        send_sem=psend.at[p, o], recv_sem=precv.at[p, o],
                        device_id=(me, giver), device_id_type=MESH).wait_recv()
        if hop >= 2:
            for dz in sorted({hop - 2, 2 - hop}):
                plane_dot(dz, hop == 2)

    def give(p):
        to = lax.rem(grp + p, n_grp)
        return pltpu.make_async_remote_copy(
            src_ref=block.at[to], dst_ref=out.at[grp], send_sem=osend.at[p], recv_sem=orecv.at[p],
            device_id=(me, to), device_id_type=MESH)

    for p in range(1, n_grp):
        to = lax.rem(grp + p, n_grp)
        block[to] = total[to].astype(block.dtype)
        give(p).start()
    block[grp] = total[grp].astype(block.dtype)
    keep = pltpu.make_async_copy(block.at[grp], out.at[grp], own_sem.at[2])
    keep.start()

    for dz, source, colour, ways in sent:
        def drain(source=source, colour=colour, ways=ways):
            for way in ways:
                when(edges[way], copy(source, colour, way).wait_send)
        if ways:
            when(valid(dz), drain)
    for o in range(1, n_aux):
        fac_copy(o).wait_send()
    for o in range(n_aux):
        source = lax.rem(me + n_aux - o, n_aux)
        for p in range(1, n_grp):
            share(o, source, p).wait_send()
    for p in range(1, n_grp):
        giver = lax.rem(grp + n_grp - p, n_grp)
        give(p).wait_send()
        pltpu.make_async_remote_copy(
            src_ref=block.at[giver], dst_ref=out.at[giver], send_sem=osend.at[p], recv_sem=orecv.at[p],
            device_id=(me, giver), device_id_type=MESH).wait_recv()
    keep.wait()


def panels(stored, chunk, n_aux, n_grp):
    depth = stored.shape[0]
    width = stored.shape[1] // n_grp
    cols = chunk.shape[2]
    dma = pltpu.SemaphoreType.DMA
    return pl.pallas_call(
        functools.partial(panel_kernel, n_aux, n_grp),
        out_shape=jax.ShapeDtypeStruct((n_grp, cols, width), jnp.bfloat16),
        in_specs=[pl.BlockSpec(memory_space=pltpu.HBM)] * 2,
        out_specs=pl.BlockSpec(memory_space=pltpu.HBM),
        scratch_shapes=[
            pltpu.VMEM((n_aux, depth, width), jnp.bfloat16),
            pltpu.VMEM((n_grp, n_aux, depth, cols), jnp.bfloat16),
            pltpu.VMEM((n_grp, cols, width), jnp.float32),
            pltpu.VMEM((n_grp, cols, width), jnp.bfloat16),
            dma((3,)),
            dma((2, n_aux)),
            dma((2, 4, n_aux)),
            dma((n_aux,)),
            dma((n_aux,)),
            dma((n_grp, n_aux)),
            dma((n_grp, n_aux)),
            dma((n_grp,)),
            dma((n_grp,)),
        ],
        compiler_params=pltpu.CompilerParams(
            collective_id=0, has_side_effects=True, vmem_limit_bytes=60 * 1024 * 1024),
    )(stored, chunk)


def make_per_device(n_aux, n_grp, v):
    def per_device(integrals, block_pairs, occupied, virtual, stored):
        nocc, nbas = occupied.shape
        aux_rows, nb, flat = integrals.shape
        slab = virtual.shape[1]
        local = slab // n_aux
        blk = 1
        while blk * blk < flat:
            blk *= 2
        pairs = block_pairs[0]
        columns = lax.all_gather(pairs[:, 1], "grp", axis=0, tiled=True)
        pick = (pairs[:, 0:1] == jnp.arange(nbas // blk, dtype=jnp.int32)[None, :])
        picked = jnp.einsum(
            "ikm,bk->ibm", occupied.reshape(nocc, nbas // blk, blk), pick.astype(jnp.bfloat16),
            preferred_element_type=jnp.float32)
        weights = jnp.broadcast_to(picked[..., None], (nocc, nb, blk, blk)).reshape(nocc, nb, flat)
        part = contract(integrals, weights, blk)
        part = part.transpose(2, 0, 1, 3).reshape(1, nb, nocc * aux_rows, blk)
        parts = lax.all_gather(part, "grp", axis=0, tiled=True)
        product = factors(parts, columns, virtual)
        chunk = product.reshape(n_grp, nocc, aux_rows, n_aux, local).transpose(3, 0, 2, 1, 4)
        chunk = chunk.reshape(n_aux, n_grp * aux_rows, nocc * local)
        panel = panels(stored, chunk, n_aux, n_grp)
        panel = panel.transpose(1, 0, 2).reshape(nocc, local, n_grp * panel.shape[2] // v, v)
        return panel

    return per_device


def solution(mesh):
    n_aux, n_grp = mesh.shape["aux"], mesh.shape["grp"]

    def whole(integrals, block_pairs, occupied, virtual, stored):
        return jax.shard_map(
            make_per_device(n_aux, n_grp, virtual.shape[1]),
            mesh=mesh,
            in_specs=(
                P(("aux", "grp"), None, None),
                P(("aux", "grp"), None, None),
                P(),
                P(None, "grp"),
                P("aux", None),
            ),
            out_specs=P(None, ("grp", "aux"), None, None),
            check_vma=False,
        )(integrals, block_pairs, occupied, virtual, stored)

    return whole
```

```python
import functools
import math

import jax
import jax.numpy as jnp
from jax import lax
from jax.experimental import pallas as pl
from jax.experimental.pallas import tpu as pltpu
from jax.sharding import PartitionSpec as P

MESH = pl.DeviceIdType.MESH
LANES = 128
PLANE = 4


def weigh(pairs, occ, weights):
    nb = pairs.shape[0]
    nocc, nblocks, blk = occ.shape
    lanes = lax.broadcasted_iota(jnp.int32, (nb, nblocks), 1)
    pick = (pairs[:, 0:1] == lanes).astype(jnp.bfloat16)
    step = 8 * LANES
    row = lax.broadcasted_iota(jnp.int32, (blk, step), 0) * blk
    col = lax.broadcasted_iota(jnp.int32, (blk, step), 1)
    for i in range(nocc):
        picked = jnp.dot(pick, occ[i], preferred_element_type=jnp.float32).astype(jnp.bfloat16)
        for t in range(weights.shape[2] // step):
            offset = col + t * step - row
            spread = ((offset >= 0) & (offset < blk)).astype(jnp.bfloat16)
            weights[i, :, t * step:(t + 1) * step] = jnp.dot(
                picked, spread, preferred_element_type=jnp.float32)


def contract(blk, integrals, weights, part):
    aux_rows = integrals.shape[0]
    nocc = weights.shape[0]

    @pl.loop(0, aux_rows)
    def _(p):
        for i in range(nocc):
            sums = [None, None]
            for t in range(integrals.shape[2] // LANES):
                cols = slice(t * LANES, (t + 1) * LANES)
                term = integrals[p, :, cols].astype(jnp.float32) * weights[i, :, cols]
                sums[t % 2] = term if sums[t % 2] is None else sums[t % 2] + term
            total = sums[0] + sums[1]
            whole = total
            for f in range(1, LANES // blk):
                whole = whole + pltpu.roll(total, f * blk, 1)
            part[i * aux_rows + p] = whole


def place(blk, pairs, part, turned, half, grp):
    nb = pairs.shape[0]
    per = LANES // blk
    for k in range(nb):
        turned[k] = part[:, k, :]
    lane = lax.broadcasted_iota(jnp.int32, (1, LANES), 1) // blk

    @pl.loop(0, half.shape[2] // LANES)
    def _(b):
        here = lane + b * per
        total = None
        for k in range(nb):
            term = jnp.where(here == pairs[k:k + 1, 1:2], turned[k], 0.0)
            total = term if total is None else total + term
        half[grp, :, pl.ds(pl.multiple_of(b * LANES, LANES), LANES)] = total.astype(half.dtype)


def multiply(nocc, local, half, virt, chunk):
    n_grp, both, nbas = half.shape
    aux_rows = both // nocc
    step = math.lcm(local, LANES)
    for t in range(virt.shape[1] // step):
        product = jnp.dot(
            half[...].reshape(n_grp * both, nbas), virt[:, t * step:(t + 1) * step],
            preferred_element_type=jnp.float32)
        for c in range(step // local):
            d = t * (step // local) + c
            for q in range(n_grp):
                for i in range(nocc):
                    top = q * both + i * aux_rows
                    chunk[d, q * aux_rows:(q + 1) * aux_rows, i * local:(i + 1) * local] = product[
                        top:top + aux_rows, c * local:(c + 1) * local].astype(chunk.dtype)


def panel_kernel(n_aux, n_grp, integrals, pairs, occ, virtual, stored, out, rows, fac, total, block,
                 ints, virt, weights, part, turned, half, chunk,
                 own_sem, recv, send, frecv, fsend, precv, psend, orecv, osend, hrecv, hsend):
    me = lax.axis_index("aux")
    grp = lax.axis_index("grp")
    line = n_aux // PLANE
    width = rows.shape[2]
    cut = width // 3 // LANES * LANES
    spans = ((0, cut), (cut, width - cut))
    z = me // PLANE
    su = 1 + grp % 2
    sv = 3 - su
    u = (me // su) % 2
    v = (me // sv) % 2
    next_u = me + su * (1 - 2 * u)
    next_v = me + sv * (1 - 2 * v)
    up, down = z + 1 < line, z >= 1
    targets = {"up": me + PLANE, "down": me - PLANE, "u": next_u, "v": next_v}
    slots = {"up": 0, "down": 1, "u": 2, "v": 3}

    load = pltpu.make_async_copy(
        stored.at[:, pl.ds(pl.multiple_of(grp * width, LANES), width)], rows.at[me], own_sem.at[0])
    load.start()
    mine = pltpu.make_async_copy(chunk.at[me], fac.at[grp, me], own_sem.at[1])
    load_ints = pltpu.make_async_copy(integrals, ints, own_sem.at[3])
    load_ints.start()
    load_virt = pltpu.make_async_copy(virtual, virt, own_sem.at[4])
    load_virt.start()
    nocc, nblocks, blk = occ.shape
    local = virtual.shape[1] // n_aux

    barrier = pltpu.get_barrier_semaphore()
    for o in range(1, n_aux):
        pl.semaphore_signal(barrier, inc=1, device_id=(lax.rem(me + o, n_aux), grp), device_id_type=MESH)
    for o in range(1, n_grp):
        pl.semaphore_signal(barrier, inc=1, device_id=(me, lax.rem(grp + o, n_grp)), device_id_type=MESH)
    pl.semaphore_wait(barrier, n_aux - 1 + n_grp - 1)

    def copy(source, colour, way):
        at = rows.at[source, :, pl.ds(*spans[colour])]
        return pltpu.make_async_remote_copy(
            src_ref=at, dst_ref=at,
            send_sem=send.at[colour, slots[way], source], recv_sem=recv.at[colour, source],
            device_id=(targets[way], grp), device_id_type=MESH)

    def when(condition, action):
        if condition is None:
            action()
        else:
            pl.when(condition)(action)

    edges = {"up": up, "down": down, "u": None, "v": None}

    def ways_of(dz, du, dv, colour):
        if dv:
            return ()
        along = ("up", "down") if dz == 0 else (("up",) if dz > 0 else ("down",))
        if colour == 0:
            return ("v",) if du else along + ("u", "v")
        if dz == 0 and du == 0:
            return ("u",) + along + ("v",)
        return along + ("v",)

    def source_of(dz, du, dv):
        return (z - dz) * PLANE + su * (u + du * (1 - 2 * u)) + sv * (v + dv * (1 - 2 * v))

    def valid(dz):
        if dz == 0:
            return None
        return z - dz >= 0 if dz > 0 else z - dz < line

    sent = []

    def forward(dz, du, dv):
        source = source_of(dz, du, dv)
        for colour in (0, 1):
            ways = ways_of(dz, du, dv, colour)
            sent.append((dz, source, colour, ways))

            def act(colour=colour, ways=ways):
                if (dz, du, dv) != (0, 0, 0):
                    copy(source, colour, "v").wait_recv()
                for way in ways:
                    when(edges[way], copy(source, colour, way).start)

            when(valid(dz), act)

    def plane_dot(dz, first):
        def act():
            base = (z - dz) * PLANE
            tile = 512 if width % 512 == 0 else LANES

            @pl.loop(0, width // tile)
            def _(t):
                cols = pl.ds(pl.multiple_of(t * tile, tile), tile)
                right = rows[pl.ds(base, PLANE), :, cols].reshape(-1, tile)
                for q in range(n_grp):
                    left = fac[q, pl.ds(base, PLANE)].reshape(-1, fac.shape[3])
                    term = lax.dot_general(
                        left, right, (((0,), (0,)), ((), ())), preferred_element_type=jnp.float32)
                    if first:
                        total[q, :, cols] = term
                    else:
                        total[q, :, cols] += term

        when(valid(dz), act)

    offsets = [(dz, du, dv) for dz in range(1 - line, line) for du in (0, 1) for dv in (0, 1)]
    hops = lambda o: abs(o[0]) + o[1] + o[2]
    last_hop = line + 1

    def fac_copy(o):
        to = lax.rem(me + o, n_aux)
        return pltpu.make_async_remote_copy(
            src_ref=chunk.at[to], dst_ref=fac.at[grp, me], send_sem=fsend.at[o], recv_sem=frecv.at[o],
            device_id=(to, grp), device_id_type=MESH)

    def fac_wait(o):
        source = lax.rem(me + n_aux - o, n_aux)
        pltpu.make_async_remote_copy(
            src_ref=chunk.at[0], dst_ref=fac.at[grp, source], send_sem=fsend.at[o], recv_sem=frecv.at[o],
            device_id=(source, grp), device_id_type=MESH).wait_recv()
        return source

    def share(o, source, p):
        return pltpu.make_async_remote_copy(
            src_ref=fac.at[grp, source], dst_ref=fac.at[grp, source],
            send_sem=psend.at[p, o], recv_sem=precv.at[p, o],
            device_id=(me, lax.rem(grp + p, n_grp)), device_id_type=MESH)

    def half_copy(p):
        return pltpu.make_async_remote_copy(
            src_ref=half.at[grp], dst_ref=half.at[grp], send_sem=hsend.at[p], recv_sem=hrecv.at[p],
            device_id=(me, lax.rem(grp + p, n_grp)), device_id_type=MESH)

    for hop in range(last_hop + 1):
        if hop == 0:
            load.wait()
        for offset in offsets:
            if hops(offset) == hop:
                forward(*offset)
        if hop == 0:
            weigh(pairs, occ, weights)
            load_ints.wait()
            contract(blk, ints, weights, part)
            place(blk, pairs, part, turned, half, grp)
            for p in range(1, n_grp):
                half_copy(p).start()
        if hop == 1:
            for p in range(1, n_grp):
                giver = lax.rem(grp + n_grp - p, n_grp)
                pltpu.make_async_remote_copy(
                    src_ref=half.at[giver], dst_ref=half.at[giver], send_sem=hsend.at[p],
                    recv_sem=hrecv.at[p], device_id=(me, giver), device_id_type=MESH).wait_recv()
            load_virt.wait()
            multiply(nocc, local, half, virt, chunk)
            mine.start()
            for o in range(1, n_aux):
                fac_copy(o).start()
            mine.wait()
        if hop == 2:
            for o in range(n_aux):
                source = me if o == 0 else fac_wait(o)
                for p in range(1, n_grp):
                    share(o, source, p).start()
            for o in range(n_aux):
                source = lax.rem(me + n_aux - o, n_aux)
                for p in range(1, n_grp):
                    giver = lax.rem(grp + n_grp - p, n_grp)
                    pltpu.make_async_remote_copy(
                        src_ref=fac.at[grp, source], dst_ref=fac.at[giver, source],
                        send_sem=psend.at[p, o], recv_sem=precv.at[p, o],
                        device_id=(me, giver), device_id_type=MESH).wait_recv()
        if hop >= 2:
            for dz in sorted({hop - 2, 2 - hop}):
                plane_dot(dz, hop == 2)

    def give(p):
        to = lax.rem(grp + p, n_grp)
        return pltpu.make_async_remote_copy(
            src_ref=block.at[to], dst_ref=out.at[grp], send_sem=osend.at[p], recv_sem=orecv.at[p],
            device_id=(me, to), device_id_type=MESH)

    for p in range(1, n_grp):
        to = lax.rem(grp + p, n_grp)
        block[to] = total[to].astype(block.dtype)
        give(p).start()
    block[grp] = total[grp].astype(block.dtype)
    keep = pltpu.make_async_copy(block.at[grp], out.at[grp], own_sem.at[2])
    keep.start()

    for dz, source, colour, ways in sent:
        def drain(source=source, colour=colour, ways=ways):
            for way in ways:
                when(edges[way], copy(source, colour, way).wait_send)
        if ways:
            when(valid(dz), drain)
    for p in range(1, n_grp):
        half_copy(p).wait_send()
    for o in range(1, n_aux):
        fac_copy(o).wait_send()
    for o in range(n_aux):
        source = lax.rem(me + n_aux - o, n_aux)
        for p in range(1, n_grp):
            share(o, source, p).wait_send()
    for p in range(1, n_grp):
        giver = lax.rem(grp + n_grp - p, n_grp)
        give(p).wait_send()
        pltpu.make_async_remote_copy(
            src_ref=block.at[giver], dst_ref=out.at[giver], send_sem=osend.at[p], recv_sem=orecv.at[p],
            device_id=(me, giver), device_id_type=MESH).wait_recv()
    keep.wait()


def panels(integrals, pairs, occ, virtual, stored, n_aux, n_grp):
    depth = stored.shape[0]
    width = stored.shape[1] // n_grp
    aux_rows, nb, flat = integrals.shape
    nocc, nblocks, blk = occ.shape
    nbas, slab = virtual.shape
    cols = nocc * (slab // n_aux)
    dma = pltpu.SemaphoreType.DMA
    hbm = pl.BlockSpec(memory_space=pltpu.HBM)
    vmem = pl.BlockSpec(memory_space=pltpu.VMEM)
    return pl.pallas_call(
        functools.partial(panel_kernel, n_aux, n_grp),
        out_shape=jax.ShapeDtypeStruct((n_grp, cols, width), jnp.bfloat16),
        in_specs=[hbm, vmem, vmem, hbm, hbm],
        out_specs=hbm,
        scratch_shapes=[
            pltpu.VMEM((n_aux, depth, width), jnp.bfloat16),
            pltpu.VMEM((n_grp, n_aux, depth, cols), jnp.bfloat16),
            pltpu.VMEM((n_grp, cols, width), jnp.float32),
            pltpu.VMEM((n_grp, cols, width), jnp.bfloat16),
            pltpu.VMEM(integrals.shape, jnp.bfloat16),
            pltpu.VMEM(virtual.shape, jnp.bfloat16),
            pltpu.VMEM((nocc, nb, flat), jnp.float32),
            pltpu.VMEM((nocc * aux_rows, nb, LANES), jnp.float32),
            pltpu.VMEM((nb, nocc * aux_rows, LANES), jnp.float32),
            pltpu.VMEM((n_grp, nocc * aux_rows, nbas), jnp.bfloat16),
            pltpu.VMEM((n_aux, depth, cols), jnp.bfloat16),
            dma((5,)),
            dma((2, n_aux)),
            dma((2, 4, n_aux)),
            dma((n_aux,)),
            dma((n_aux,)),
            dma((n_grp, n_aux)),
            dma((n_grp, n_aux)),
            dma((n_grp,)),
            dma((n_grp,)),
            dma((n_grp,)),
            dma((n_grp,)),
        ],
        compiler_params=pltpu.CompilerParams(
            collective_id=0, has_side_effects=True, vmem_limit_bytes=63 * 1024 * 1024),
    )(integrals, pairs, occ, virtual, stored)


def make_per_device(n_aux, n_grp, v):
    def per_device(integrals, block_pairs, occupied, virtual, stored):
        nocc, nbas = occupied.shape
        local = virtual.shape[1] // n_aux
        blk = math.isqrt(integrals.shape[2])
        occ = occupied.reshape(nocc, nbas // blk, blk)
        panel = panels(integrals, block_pairs[0], occ, virtual, stored, n_aux, n_grp)
        return panel.transpose(1, 0, 2).reshape(nocc, local, n_grp * panel.shape[2] // v, v)

    return per_device


def solution(mesh):
    n_aux, n_grp = mesh.shape["aux"], mesh.shape["grp"]

    def whole(integrals, block_pairs, occupied, virtual, stored):
        return jax.shard_map(
            make_per_device(n_aux, n_grp, virtual.shape[1]),
            mesh=mesh,
            in_specs=(
                P(("aux", "grp"), None, None),
                P(("aux", "grp"), None, None),
                P(),
                P(None, "grp"),
                P("aux", None),
            ),
            out_specs=P(None, ("grp", "aux"), None, None),
            check_vma=False,
        )(integrals, block_pairs, occupied, virtual, stored)

    return whole
```

```python
import functools
import math

import jax
import jax.numpy as jnp
from jax import lax
from jax.experimental import pallas as pl
from jax.experimental.pallas import tpu as pltpu
from jax.sharding import PartitionSpec as P

MESH = pl.DeviceIdType.MESH
LANES = 128
PLANE = 4
PIECES = 3
FIRST = 1


def spans_of(width):
    piece = width // PIECES // LANES * LANES
    starts = [n * piece for n in range(PIECES)] + [width]
    return [(a, b - a, 0 if n < FIRST else 1) for n, (a, b) in enumerate(zip(starts, starts[1:]))]


def weigh(pairs, occ, weights):
    nb = pairs.shape[0]
    nocc, nblocks, blk = occ.shape
    lanes = lax.broadcasted_iota(jnp.int32, (nb, nblocks), 1)
    pick = (pairs[:, 0:1] == lanes).astype(jnp.bfloat16)
    step = 8 * LANES
    row = lax.broadcasted_iota(jnp.int32, (blk, step), 0) * blk
    col = lax.broadcasted_iota(jnp.int32, (blk, step), 1)
    for i in range(nocc):
        picked = jnp.dot(pick, occ[i], preferred_element_type=jnp.float32).astype(jnp.bfloat16)
        for t in range(weights.shape[2] // step):
            offset = col + t * step - row
            spread = ((offset >= 0) & (offset < blk)).astype(jnp.bfloat16)
            weights[i, :, t * step:(t + 1) * step] = jnp.dot(
                picked, spread, preferred_element_type=jnp.float32)


def contract(blk, integrals, weights, part):
    aux_rows = integrals.shape[0]
    nocc = weights.shape[0]

    @pl.loop(0, aux_rows)
    def _(p):
        for i in range(nocc):
            sums = [None, None]
            for t in range(integrals.shape[2] // LANES):
                cols = slice(t * LANES, (t + 1) * LANES)
                term = integrals[p, :, cols].astype(jnp.float32) * weights[i, :, cols]
                sums[t % 2] = term if sums[t % 2] is None else sums[t % 2] + term
            total = sums[0] + sums[1]
            whole = total
            for f in range(1, LANES // blk):
                whole = whole + pltpu.roll(total, f * blk, 1)
            part[i * aux_rows + p] = whole


def place(blk, pairs, part, turned, half, grp):
    nb = pairs.shape[0]
    per = LANES // blk
    for k in range(nb):
        turned[k] = part[:, k, :]
    lane = lax.broadcasted_iota(jnp.int32, (1, LANES), 1) // blk

    @pl.loop(0, half.shape[2] // LANES)
    def _(b):
        here = lane + b * per
        total = None
        for k in range(nb):
            term = jnp.where(here == pairs[k:k + 1, 1:2], turned[k], 0.0)
            total = term if total is None else total + term
        half[grp, :, pl.ds(pl.multiple_of(b * LANES, LANES), LANES)] = total.astype(half.dtype)


def multiply(nocc, local, half, virt, chunk):
    n_grp, both, nbas = half.shape
    aux_rows = both // nocc
    step = math.lcm(local, LANES)
    for t in range(virt.shape[1] // step):
        product = jnp.dot(
            half[...].reshape(n_grp * both, nbas), virt[:, t * step:(t + 1) * step],
            preferred_element_type=jnp.float32)
        for c in range(step // local):
            d = t * (step // local) + c
            for q in range(n_grp):
                for i in range(nocc):
                    top = q * both + i * aux_rows
                    chunk[d, q * aux_rows:(q + 1) * aux_rows, i * local:(i + 1) * local] = product[
                        top:top + aux_rows, c * local:(c + 1) * local].astype(chunk.dtype)


def panel_kernel(n_aux, n_grp, integrals, pairs_in, occ, virtual, stored, out, rows, fac, total, block,
                 ints, virt, weights, part, turned, half, chunk,
                 own_sem, recv, send, frecv, fsend, precv, psend, orecv, osend, hrecv, hsend):
    me = lax.axis_index("aux")
    grp = lax.axis_index("grp")
    line = n_aux // PLANE
    width = rows.shape[2]
    spans = spans_of(width)
    z = me // PLANE
    su = 1 + grp % 2
    sv = 3 - su
    u = (me // su) % 2
    v = (me // sv) % 2
    next_u = me + su * (1 - 2 * u)
    next_v = me + sv * (1 - 2 * v)
    up, down = z + 1 < line, z >= 1
    targets = {"up": me + PLANE, "down": me - PLANE, "u": next_u, "v": next_v}
    slots = {"up": 0, "down": 1, "u": 2, "v": 3}

    load = pltpu.make_async_copy(
        stored.at[:, pl.ds(pl.multiple_of(grp * width, LANES), width)], rows.at[me], own_sem.at[0])
    load.start()
    mine = pltpu.make_async_copy(chunk.at[me], fac.at[grp, me], own_sem.at[1])
    load_ints = pltpu.make_async_copy(integrals, ints, own_sem.at[3])
    load_ints.start()
    load_virt = pltpu.make_async_copy(virtual, virt, own_sem.at[4])
    load_virt.start()
    pairs = pairs_in.at[0]
    nocc, nblocks, blk = occ.shape
    local = virtual.shape[1] // n_aux

    barrier = pltpu.get_barrier_semaphore()
    for o in range(1, n_aux):
        pl.semaphore_signal(barrier, inc=1, device_id=(lax.rem(me + o, n_aux), grp), device_id_type=MESH)
    for o in range(1, n_grp):
        pl.semaphore_signal(barrier, inc=1, device_id=(me, lax.rem(grp + o, n_grp)), device_id_type=MESH)
    pl.semaphore_wait(barrier, n_aux - 1 + n_grp - 1)

    def copy(source, colour, way):
        at = rows.at[source, :, pl.ds(*spans[colour][:2])]
        return pltpu.make_async_remote_copy(
            src_ref=at, dst_ref=at,
            send_sem=send.at[colour, slots[way], source], recv_sem=recv.at[colour, source],
            device_id=(targets[way], grp), device_id_type=MESH)

    def when(condition, action):
        if condition is None:
            action()
        else:
            pl.when(condition)(action)

    edges = {"up": up, "down": down, "u": None, "v": None}

    def ways_of(dz, du, dv, colour):
        if dv:
            return ()
        along = ("up", "down") if dz == 0 else (("up",) if dz > 0 else ("down",))
        if colour == 0:
            return ("v",) if du else along + ("u", "v")
        if dz == 0 and du == 0:
            return ("u",) + along + ("v",)
        return along + ("v",)

    def source_of(dz, du, dv):
        return (z - dz) * PLANE + su * (u + du * (1 - 2 * u)) + sv * (v + dv * (1 - 2 * v))

    def valid(dz):
        if dz == 0:
            return None
        return z - dz >= 0 if dz > 0 else z - dz < line

    sent = []

    def forward(dz, du, dv):
        source = source_of(dz, du, dv)
        for colour in range(len(spans)):
            ways = ways_of(dz, du, dv, spans[colour][2])
            sent.append((dz, source, colour, ways))

            def act(colour=colour, ways=ways):
                if (dz, du, dv) != (0, 0, 0):
                    copy(source, colour, "v").wait_recv()
                for way in ways:
                    when(edges[way], copy(source, colour, way).start)

            when(valid(dz), act)

    def plane_dot(dz, first):
        def act():
            base = (z - dz) * PLANE
            tile = 512 if width % 512 == 0 else LANES

            @pl.loop(0, width // tile)
            def _(t):
                cols = pl.ds(pl.multiple_of(t * tile, tile), tile)
                right = rows[pl.ds(base, PLANE), :, cols].reshape(-1, tile)
                for q in range(n_grp):
                    left = fac[q, pl.ds(base, PLANE)].reshape(-1, fac.shape[3])
                    term = lax.dot_general(
                        left, right, (((0,), (0,)), ((), ())), preferred_element_type=jnp.float32)
                    if first:
                        total[q, :, cols] = term
                    else:
                        total[q, :, cols] += term

        when(valid(dz), act)

    offsets = [(dz, du, dv) for dz in range(1 - line, line) for du in (0, 1) for dv in (0, 1)]
    hops = lambda o: abs(o[0]) + o[1] + o[2]
    last_hop = line + 1

    def fac_copy(o):
        to = lax.rem(me + o, n_aux)
        return pltpu.make_async_remote_copy(
            src_ref=chunk.at[to], dst_ref=fac.at[grp, me], send_sem=fsend.at[o], recv_sem=frecv.at[o],
            device_id=(to, grp), device_id_type=MESH)

    def fac_wait(o):
        source = lax.rem(me + n_aux - o, n_aux)
        pltpu.make_async_remote_copy(
            src_ref=chunk.at[0], dst_ref=fac.at[grp, source], send_sem=fsend.at[o], recv_sem=frecv.at[o],
            device_id=(source, grp), device_id_type=MESH).wait_recv()
        return source

    def share(o, source, p):
        return pltpu.make_async_remote_copy(
            src_ref=fac.at[grp, source], dst_ref=fac.at[grp, source],
            send_sem=psend.at[p, o], recv_sem=precv.at[p, o],
            device_id=(me, lax.rem(grp + p, n_grp)), device_id_type=MESH)

    def half_copy(p):
        return pltpu.make_async_remote_copy(
            src_ref=half.at[grp], dst_ref=half.at[grp], send_sem=hsend.at[p], recv_sem=hrecv.at[p],
            device_id=(me, lax.rem(grp + p, n_grp)), device_id_type=MESH)

    for hop in range(last_hop + 1):
        if hop == 0:
            load.wait()
        for offset in offsets:
            if hops(offset) == hop:
                forward(*offset)
        if hop == 0:
            weigh(pairs, occ, weights)
            load_ints.wait()
            contract(blk, ints, weights, part)
            place(blk, pairs, part, turned, half, grp)
            for p in range(1, n_grp):
                half_copy(p).start()
        if hop == 1:
            for p in range(1, n_grp):
                giver = lax.rem(grp + n_grp - p, n_grp)
                pltpu.make_async_remote_copy(
                    src_ref=half.at[giver], dst_ref=half.at[giver], send_sem=hsend.at[p],
                    recv_sem=hrecv.at[p], device_id=(me, giver), device_id_type=MESH).wait_recv()
            load_virt.wait()
            multiply(nocc, local, half, virt, chunk)
            mine.start()
            for o in range(1, n_aux):
                fac_copy(o).start()
            mine.wait()
        if hop == 2:
            for o in range(n_aux):
                source = me if o == 0 else fac_wait(o)
                for p in range(1, n_grp):
                    share(o, source, p).start()
            for o in range(n_aux):
                source = lax.rem(me + n_aux - o, n_aux)
                for p in range(1, n_grp):
                    giver = lax.rem(grp + n_grp - p, n_grp)
                    pltpu.make_async_remote_copy(
                        src_ref=fac.at[grp, source], dst_ref=fac.at[giver, source],
                        send_sem=psend.at[p, o], recv_sem=precv.at[p, o],
                        device_id=(me, giver), device_id_type=MESH).wait_recv()
        if hop >= 2:
            for dz in sorted({hop - 2, 2 - hop}):
                plane_dot(dz, hop == 2)

    def give(p, n):
        to = lax.rem(grp + p, n_grp)
        cols = pl.ds(*spans[n][:2])
        return pltpu.make_async_remote_copy(
            src_ref=block.at[to, :, cols], dst_ref=out.at[grp, :, cols],
            send_sem=osend.at[p, n], recv_sem=orecv.at[p, n],
            device_id=(me, to), device_id_type=MESH)

    for p in range(1, n_grp):
        to = lax.rem(grp + p, n_grp)
        for n in range(len(spans)):
            cols = pl.ds(*spans[n][:2])
            block[to, :, cols] = total[to, :, cols].astype(block.dtype)
            give(p, n).start()
    block[grp] = total[grp].astype(block.dtype)
    keep = pltpu.make_async_copy(block.at[grp], out.at[grp], own_sem.at[2])
    keep.start()

    for dz, source, colour, ways in sent:
        def drain(source=source, colour=colour, ways=ways):
            for way in ways:
                when(edges[way], copy(source, colour, way).wait_send)
        if ways:
            when(valid(dz), drain)
    for p in range(1, n_grp):
        half_copy(p).wait_send()
    for o in range(1, n_aux):
        fac_copy(o).wait_send()
    for o in range(n_aux):
        source = lax.rem(me + n_aux - o, n_aux)
        for p in range(1, n_grp):
            share(o, source, p).wait_send()
    for p in range(1, n_grp):
        giver = lax.rem(grp + n_grp - p, n_grp)
        for n in range(len(spans)):
            cols = pl.ds(*spans[n][:2])
            give(p, n).wait_send()
            pltpu.make_async_remote_copy(
                src_ref=block.at[giver, :, cols], dst_ref=out.at[giver, :, cols],
                send_sem=osend.at[p, n], recv_sem=orecv.at[p, n],
                device_id=(me, giver), device_id_type=MESH).wait_recv()
    keep.wait()


def panels(integrals, pairs, occ, virtual, stored, n_aux, n_grp):
    depth = stored.shape[0]
    width = stored.shape[1] // n_grp
    aux_rows, nb, flat = integrals.shape
    nocc, nblocks, blk = occ.shape
    nbas, slab = virtual.shape
    pieces = len(spans_of(width))
    cols = nocc * (slab // n_aux)
    dma = pltpu.SemaphoreType.DMA
    hbm = pl.BlockSpec(memory_space=pltpu.HBM)
    vmem = pl.BlockSpec(memory_space=pltpu.VMEM)
    return pl.pallas_call(
        functools.partial(panel_kernel, n_aux, n_grp),
        out_shape=jax.ShapeDtypeStruct((n_grp, cols, width), jnp.bfloat16),
        in_specs=[hbm, vmem, vmem, hbm, hbm],
        out_specs=hbm,
        scratch_shapes=[
            pltpu.VMEM((n_aux, depth, width), jnp.bfloat16),
            pltpu.VMEM((n_grp, n_aux, depth, cols), jnp.bfloat16),
            pltpu.VMEM((n_grp, cols, width), jnp.float32),
            pltpu.VMEM((n_grp, cols, width), jnp.bfloat16),
            pltpu.VMEM(integrals.shape, jnp.bfloat16),
            pltpu.VMEM(virtual.shape, jnp.bfloat16),
            pltpu.VMEM((nocc, nb, flat), jnp.float32),
            pltpu.VMEM((nocc * aux_rows, nb, LANES), jnp.float32),
            pltpu.VMEM((nb, nocc * aux_rows, LANES), jnp.float32),
            pltpu.VMEM((n_grp, nocc * aux_rows, nbas), jnp.bfloat16),
            pltpu.VMEM((n_aux, depth, cols), jnp.bfloat16),
            dma((5,)),
            dma((pieces, n_aux)),
            dma((pieces, 4, n_aux)),
            dma((n_aux,)),
            dma((n_aux,)),
            dma((n_grp, n_aux)),
            dma((n_grp, n_aux)),
            dma((n_grp, pieces)),
            dma((n_grp, pieces)),
            dma((n_grp,)),
            dma((n_grp,)),
        ],
        compiler_params=pltpu.CompilerParams(
            collective_id=0, has_side_effects=True, vmem_limit_bytes=63 * 1024 * 1024),
    )(integrals, pairs, occ, virtual, stored)


def make_per_device(n_aux, n_grp, v):
    def per_device(integrals, block_pairs, occupied, virtual, stored):
        nocc, nbas = occupied.shape
        local = virtual.shape[1] // n_aux
        blk = math.isqrt(integrals.shape[2])
        occ = occupied.reshape(nocc, nbas // blk, blk)
        panel = panels(integrals, block_pairs, occ, virtual, stored, n_aux, n_grp)
        return panel.transpose(1, 0, 2).reshape(nocc, local, n_grp * panel.shape[2] // v, v)

    return per_device


def solution(mesh):
    n_aux, n_grp = mesh.shape["aux"], mesh.shape["grp"]

    def whole(integrals, block_pairs, occupied, virtual, stored):
        return jax.shard_map(
            make_per_device(n_aux, n_grp, virtual.shape[1]),
            mesh=mesh,
            in_specs=(
                P(("aux", "grp"), None, None),
                P(("aux", "grp"), None, None),
                P(),
                P(None, "grp"),
                P("aux", None),
            ),
            out_specs=P(None, ("grp", "aux"), None, None),
            check_vma=False,
        )(integrals, block_pairs, occupied, virtual, stored)

    return whole
```
